32 devices in a mesh: group: 2 (over y), head: 4 (over x, core), st: 4 (over z).
Axes of the slice: x: 2, y: 2, z: 4, core: 2. Of those that a mesh axis runs over, the one named last changes fastest.
Arguments:
- qkv_rows: bfloat16 [12288, 3, 3072], P(('group', 'st'), None, 'head'), parts along dimension 0, may hold values from -6 to 6
- out_weight: bfloat16 [3072, 3072], P('head'), may hold values from -0.15625 to 0.15625
- residual: bfloat16 [12288, 3072], P(('group', 'st'), 'head'), parts along dimension 0, may hold values from -3 to 3
- source: int32 [12288], P(('group', 'st')), parts along dimension 0, may hold values from 0 to 6143, as said below
- target: int32 [12288], P(('group', 'st')), parts along dimension 0, may hold values from 0 to 6143, as said below
- window_first: int32 [12288], P(('group', 'st')), parts along dimension 0, may hold values from 0 to 5760, as said below
Outputs:
- layer_out: bfloat16 [12288, 3072], P(('group', 'st'), 'head'), parts along dimension 0
The draws below stay inside these ranges and needn't reach their ends.
There are 2 independent parts, one for each index of `group`. The reference program is written for one: setup_inputs(seed, part) draws one part's arguments, and reference() takes and returns one part's arrays. A program takes and returns all parts, laid end to end along the dimension named above; an argument that names none is the same for every part. Nothing has to cross between parts.
Inputs may be any that keep to these rules, and one draw needn't show every extreme that they name: `source`: A permutation of the tokens that moves aligned tiles of 64 rows whole and in order. Tile t of every st device's shifted rows comes from the st device a fixed offset further along the axis (cyclically), the offset depending on t only; one st device sends at most 6 tiles to one st device, and exactly 6 to one of them. `target`: the inverse of source. `window_first`: windows are runs of whole aligned tiles inside one st device's 1536 shifted rows, of 384 to 1536 rows; in every draw some window fills all 1536 rows of a device.
All inputs are finite; a program needn't handle non-finite values.
Results may differ from the reference program's by a relative error of at most 0.0095.
Values may be sent and summed in bfloat16 or wider, within the bound.
A program may use at most 128 MiB of HBM per device.

```python
import math
import jax
import jax.numpy as jnp
from jax import lax

D = 3072
HEADS = 24
HD = 128
TOK_DEV = 1536
BLK = 64
MINB = 6
TOKENS = 6144
CAP_BLK = 6
N_HEAD = 4
N_ST = 4


def routing(key):
    dev_count = TOKENS // TOK_DEV
    tile_count = TOK_DEV // BLK
    base_key = jax.random.fold_in(key, 7001)
    star_key, others_key, order_key, cut_key, large_key = jax.random.split(base_key, 5)
    star_off = jax.random.randint(star_key, (), 0, dev_count).astype(jnp.int32)
    others = jnp.arange((dev_count - 1) * CAP_BLK, dtype=jnp.int32) // CAP_BLK
    others = others + (others >= star_off).astype(jnp.int32)
    others = jax.random.permutation(others_key, others)
    offsets = jnp.concatenate([jnp.full((CAP_BLK,), star_off, jnp.int32), others])[:tile_count]
    tile_order = jax.random.permutation(order_key, tile_count).astype(jnp.int32)
    device_ids = jnp.arange(dev_count, dtype=jnp.int32)
    src_dev = (device_ids[:, None] + offsets[None, :]) % dev_count
    src_tile = src_dev * tile_count + tile_order[None, :]
    row_ids = jnp.arange(BLK, dtype=jnp.int32)
    source = (src_tile[:, :, None] * BLK + row_ids[None, None, :]).reshape(-1)
    target = jnp.zeros_like(source).at[source].set(jnp.arange(dev_count * tile_count * BLK, dtype=jnp.int32))
    cut_bits = jax.random.randint(cut_key, (dev_count, tile_count), 0, 2).astype(jnp.int32)
    large_dev = jax.random.randint(large_key, (), 0, dev_count - 1).astype(jnp.int32)
    cut_bits = jnp.where(device_ids[:, None] == large_dev, 0, cut_bits)
    tile_ids = jnp.arange(tile_count, dtype=jnp.int32)[None, :]
    last_dev = device_ids[:, None] == dev_count - 1
    quiet = (tile_ids > tile_count - 2 * MINB) & (tile_ids < tile_count - MINB)
    cut_bits = jnp.where(last_dev & quiet, 0, cut_bits)
    cut_bits = jnp.where(last_dev & (tile_ids == tile_count - MINB), 1, cut_bits)

    def walk_tiles(state_pair, step_in):
        run_length, win_first = state_pair
        bit_now, tile_now = step_in
        do_cut = (run_length >= MINB) & (tile_count - tile_now >= MINB) & (bit_now == 1)
        win_first = jnp.where(do_cut, tile_now, win_first)
        run_length = jnp.where(do_cut, 1, run_length + 1)
        return ((run_length, win_first), win_first)
    start_pair = (jnp.zeros((dev_count,), jnp.int32), jnp.zeros((dev_count,), jnp.int32))
    _, tile_firsts = lax.scan(walk_tiles, start_pair, (cut_bits.T, jnp.arange(tile_count, dtype=jnp.int32)))
    tile_firsts = tile_firsts.T
    first_rows = (device_ids[:, None] * tile_count + tile_firsts) * BLK
    window_first = jnp.repeat(first_rows, BLK, axis=1).reshape(-1).astype(jnp.int32)
    return (source, target, window_first)


def draw_source(key, part):
    return routing(key)[0]


def draw_target(key, part):
    return routing(key)[1]


def draw_window_first(key, part):
    return routing(key)[2]


def draw_qkv_rows(key, part):
    source, target, window_first = routing(key)
    feat_cols = HEADS * HD
    value_key = jax.random.fold_in(jax.random.fold_in(key, 7003), 0)
    spread = jnp.array([1.6, 1.6, 1.0], jnp.float32).reshape(1, 3, 1)
    base_rows = jnp.clip(jax.random.normal(value_key, (TOKENS, 3, feat_cols), jnp.float32) * spread, -6.0, 6.0)
    return base_rows[target].astype(jnp.bfloat16)


def strengthened(values, rng, source, target, blocks, factor):
    owner, partner = [(jnp.arange(values.shape[axis_at]) // (values.shape[axis_at] // blocks)).reshape([-1 if axis == axis_at else 1 for axis in range(values.ndim)]) for axis_at in (source, target)]
    chosen = jax.random.permutation(rng, blocks)[partner]
    strong = (owner == chosen) | (owner == (partner + blocks // 2) % blocks)
    return jnp.where(strong, factor * values, values)


def block_levels(own_key, shape, pieces, least, high):
    def one(dim, blocks):
        draws = jax.random.uniform(jax.random.fold_in(jax.random.fold_in(own_key, 6), dim), (blocks,), jnp.float32, least / len(pieces), high / len(pieces))
        return jnp.repeat(jnp.exp(draws), shape[dim] // blocks).reshape((-1,) + (1,) * (len(shape) - dim - 1))

    factor_of = one(*pieces[0])
    for cut in pieces[1:]:
        factor_of = factor_of * one(*cut)
    return factor_of


def scatter_about(own_key, dims, width, reach, pieces=(), held_as=jnp.bfloat16):
    drawn = width * jax.random.normal(own_key, dims, jnp.float32)
    if pieces:
        drawn = drawn * block_levels(own_key, dims, pieces, -0.22, 0.18)
    return jnp.clip(drawn, -reach, reach).astype(held_as)


def gaussian_with(stream_key, extent, deviation, bound, cuts, heavy, kind=jnp.bfloat16):
    entries = deviation * jax.random.normal(stream_key, extent, jnp.float32)
    if cuts:
        entries = entries * block_levels(stream_key, extent, cuts, -0.22, 0.18)
    return jnp.clip(strengthened(entries, jax.random.fold_in(stream_key, 3), *heavy), -bound, bound).astype(kind)


def setup_inputs(seed: int = 0, part: int = 0) -> dict:
    splits = jax.random.split(jax.random.key(seed), 7)
    part_splits = jax.random.split(jax.random.fold_in(splits[6], part), 7)
    qkv_rows = draw_qkv_rows(jax.random.fold_in(jax.random.fold_in(splits[6], part), 71), part)
    out_weight = gaussian_with(splits[1], (HEADS * HD, D), (HEADS * HD) ** -0.5, 0.15625, ((0, 4),), (0, 1, 4, 2.0))
    residual = scatter_about(part_splits[2], (TOKENS, D), 0.5, 3.0, ((0, 4), (1, 4)))
    source = draw_source(jax.random.fold_in(jax.random.fold_in(splits[6], part), 71), part)
    target = draw_target(jax.random.fold_in(jax.random.fold_in(splits[6], part), 71), part)
    window_first = draw_window_first(jax.random.fold_in(jax.random.fold_in(splits[6], part), 71), part)
    return {"qkv_rows": qkv_rows, "out_weight": out_weight, "residual": residual, "source": source, "target": target, "window_first": window_first}


def attend_block(block_rows, block_first):
    row_count = block_rows.shape[0]
    queries = block_rows[:, 0].astype(jnp.float32).reshape(row_count, HEADS, HD)
    key_rows = block_rows[:, 1].astype(jnp.float32).reshape(row_count, HEADS, HD)
    value_rows = block_rows[:, 2].astype(jnp.float32).reshape(row_count, HEADS, HD)
    scores = jnp.einsum('phd,rhd->hpr', queries, key_rows) / math.sqrt(HD)
    same_window = (block_first[:, None] == block_first[None, :])[None]
    scores = jnp.where(same_window, scores, -1e+30)
    row_max = lax.optimization_barrier(jnp.max(scores, axis=2, keepdims=True))
    expo = jnp.where(same_window, jnp.exp(scores - row_max), 0.0)
    denom = lax.optimization_barrier(jnp.sum(expo, axis=2))
    weights = lax.optimization_barrier(expo.astype(jnp.bfloat16)).astype(jnp.float32)
    numer = jnp.einsum('hpr,rhd->hpd', weights, value_rows)
    result = numer / denom[..., None]
    return jnp.transpose(result, (1, 0, 2)).reshape(row_count, HEADS * HD).astype(jnp.bfloat16)

def reference(qkv_rows, out_weight, residual, source, target, window_first):
    shifted = qkv_rows[source]
    blocks = shifted.reshape(N_ST, TOK_DEV, 3, HEADS * HD)
    firsts = window_first.reshape(N_ST, TOK_DEV)
    attended = lax.map(lambda pair: attend_block(pair[0], pair[1]), (blocks, firsts))
    attended = attended.reshape(TOKENS, HEADS * HD)
    attn_home = attended[target]
    group_cols = HEADS * HD // N_HEAD
    columns = attn_home.reshape(TOKENS, N_HEAD, group_cols)
    weight_groups = out_weight.reshape(N_HEAD, group_cols, D)

    def add_group(running, group_id):
        cols_in = lax.dynamic_index_in_dim(columns, group_id, 1, keepdims=False)
        rows_in = lax.dynamic_index_in_dim(weight_groups, group_id, 0, keepdims=False)
        partial_term = jnp.dot(cols_in, rows_in, preferred_element_type=jnp.float32)
        rounded = lax.optimization_barrier(partial_term.astype(jnp.bfloat16))
        return (running + rounded.astype(jnp.float32), None)
    projected, _ = lax.scan(add_group, jnp.zeros((TOKENS, D), jnp.float32), jnp.arange(N_HEAD, dtype=jnp.int32))
    return (residual.astype(jnp.float32) + projected).astype(jnp.bfloat16)
```

```python
import functools
import math

import jax
import jax.numpy as jnp
from jax import lax
from jax.experimental import pallas as pl
from jax.experimental.pallas import tpu as pltpu
from jax.sharding import PartitionSpec as P

HD = 128
BLK = 64
FAR = 16384.0
MESH = pl.DeviceIdType.MESH


def layer_kernel(
    dims,
    order_ref,
    wid_ref,
    slot_ref,
    qkv_ref,
    w_ref,
    out_ref,
    qbuf0,
    qbuf1,
    packed,
    recv,
    att,
    home,
    wbuf,
    acc,
    q_tag,
    k_tag,
    load_sem,
    wl_sem,
    qs,
    qr,
    rs,
    rr,
    gs,
    gr,
    ws,
    wr,
):
    n_st, n_head, heads, tiles, cap, cols = dims
    rows = cap * BLK
    total = n_st * rows
    my_st = lax.axis_index("st")
    my_head = lax.axis_index("head")

    def st_peer(step):
        return {"st": lax.rem(my_st + step + n_st, n_st)}

    def head_peer(step):
        return {"head": lax.rem(my_head + step + n_head, n_head)}

    qbufs = (qbuf0, qbuf1)

    def load_copy(j, side):
        return pltpu.make_async_copy(
            qkv_ref.at[:, :, :, pl.ds(pl.multiple_of(j * HD, HD), HD)],
            qbufs[side],
            load_sem.at[side],
        )

    def send_copy(j, step):
        part = pl.ds(step * rows, rows)
        return pltpu.make_async_remote_copy(
            src_ref=packed.at[j, :, part, :],
            dst_ref=recv.at[j, :, part, :],
            send_sem=qs.at[j, step - 1],
            recv_sem=qr.at[j, step - 1],
            device_id=st_peer(step),
            device_id_type=MESH,
        )

    def return_copy(j, step):
        part = pl.ds(step * rows, rows)
        return pltpu.make_async_remote_copy(
            src_ref=att.at[j, part, :],
            dst_ref=home.at[j, part, pl.ds(0, HD)],
            send_sem=rs.at[j, step - 1],
            recv_sem=rr.at[j, step - 1],
            device_id=st_peer(-step),
            device_id_type=MESH,
        )

    def gather_copy(j, step):
        return pltpu.make_async_remote_copy(
            src_ref=home.at[j, :, pl.ds(0, HD)],
            dst_ref=home.at[j, :, pl.ds(step * HD, HD)],
            send_sem=gs.at[j, step - 1],
            recv_sem=gr.at[j, step - 1],
            device_id=head_peer(step),
            device_id_type=MESH,
        )

    def weight_cols(step):
        owner = lax.rem(my_head + step, n_head)
        return w_ref.at[:, :, pl.ds(pl.multiple_of(owner * cols, HD), cols)]

    def weight_copy(step):
        return pltpu.make_async_remote_copy(
            src_ref=weight_cols(step),
            dst_ref=wbuf.at[:, pl.ds(step * HD, HD), :],
            send_sem=ws.at[step - 1],
            recv_sem=wr.at[step - 1],
            device_id=head_peer(step),
            device_id_type=MESH,
        )

    own_weight = pltpu.make_async_copy(weight_cols(0), wbuf.at[:, pl.ds(0, HD), :], wl_sem)

    def pack(j, side):
        load_copy(j, side).wait()
        qbuf = qbufs[side]

        def own_tile(s, carry):
            tile = order_ref[s]
            for part in range(3):
                recv[j, part, pl.ds(pl.multiple_of(s * BLK, BLK), BLK), :] = qbuf[part, tile]
            return carry

        def away_tile(s, carry):
            tile = order_ref[s]
            for part in range(3):
                packed[j, part, pl.ds(pl.multiple_of(s * BLK, BLK), BLK), :] = qbuf[part, tile]
            return carry

        lax.fori_loop(0, cap, own_tile, 0)
        lax.fori_loop(cap, n_st * cap, away_tile, 0)

    def send(j):
        for step in range(1, n_st):
            send_copy(j, step).start()

    depth = min(2, heads)
    for j in range(depth):
        load_copy(j, j % 2).start()
    own_weight.start()

    barrier = pltpu.get_barrier_semaphore()
    for step in range(1, n_st):
        pl.semaphore_signal(barrier, inc=1, device_id=st_peer(step), device_id_type=MESH)
    for step in range(1, n_head):
        pl.semaphore_signal(barrier, inc=1, device_id=head_peer(step), device_id_type=MESH)

    pack(0, 0)
    pl.semaphore_wait(barrier, n_st + n_head - 2)
    send(0)
    for j in range(1, depth):
        pack(j, j % 2)
        send(j)
    for step in range(1, n_head):
        weight_copy(step).start()
    for j in range(depth, min(depth + 2, heads)):
        load_copy(j, j % 2).start()

    lane = lax.broadcasted_iota(jnp.int32, (BLK, HD), 1)

    def tag(s, carry):
        hit = lane == wid_ref[s]
        at = pl.ds(pl.multiple_of(s * BLK, BLK), BLK)
        q_tag[at, :] = jnp.where(hit, 1.0, 0.0).astype(jnp.bfloat16)
        k_tag[at, :] = jnp.where(hit, 0.0, -FAR).astype(jnp.bfloat16)
        return carry

    lax.fori_loop(0, n_st * cap, tag, 0)
    scale = math.log2(math.e) / math.sqrt(HD)
    q_rows = 256

    def attend(j):
        def q_step(block, carry):
            at = pl.ds(pl.multiple_of(block * q_rows, q_rows), q_rows)
            q = jnp.concatenate([recv[j, 0, at, :], q_tag[at, :]], axis=1)
            k = jnp.concatenate([recv[j, 1], k_tag[...]], axis=1)
            v = jnp.concatenate([recv[j, 2], jnp.ones((total, HD), jnp.bfloat16)], axis=1)
            scores = lax.dot_general(
                q, k, (((1,), (1,)), ((), ())), preferred_element_type=jnp.float32
            )
            row_max = jnp.max(scores, axis=1, keepdims=True)
            weights = jnp.exp2((scores - row_max) * scale).astype(jnp.bfloat16)
            both = jnp.dot(weights, v, preferred_element_type=jnp.float32)
            att[j, at, :] = (both[:, :HD] / both[:, HD:]).astype(jnp.bfloat16)
            return carry

        lax.fori_loop(0, total // q_rows, q_step, 0)
        home[j, pl.ds(0, rows), pl.ds(0, HD)] = att[j, pl.ds(0, rows), :]

    def project(j):
        def row_step(block, carry):
            at = pl.ds(pl.multiple_of(block * rows, rows), rows)
            term = jnp.dot(home[j, at, :], wbuf[j], preferred_element_type=jnp.float32)
            acc[pl.ds(block * cap, cap)] += term.reshape(cap, BLK, cols)
            return carry

        lax.fori_loop(0, n_st, row_step, 0)

    acc[...] = jnp.zeros_like(acc)

    def pipeline(t, carry):
        for side in range(2):

            @pl.when((t + depth < heads) & (lax.rem(t + depth, 2) == side))
            def _():
                pack(t + depth, side)
                send(t + depth)

                @pl.when(t + depth + 2 < heads)
                def _():
                    load_copy(t + depth + 2, side).start()

        @pl.when(t < heads)
        def _():
            for step in range(1, n_st):
                send_copy(t, step).wait_recv()
            attend(t)
            for step in range(1, n_st):
                return_copy(t, step).start()

        @pl.when((t >= 1) & (t <= heads))
        def _():
            for step in range(1, n_st):
                return_copy(t - 1, step).wait_recv()
            for step in range(1, n_head):
                gather_copy(t - 1, step).start()

        @pl.when(t == 2)
        def _():
            own_weight.wait()
            for step in range(1, n_head):
                weight_copy(step).wait()

        @pl.when(t >= 2)
        def _():
            for step in range(1, n_head):
                gather_copy(t - 2, step).wait_recv()
            project(t - 2)

        return carry

    lax.fori_loop(0, heads + 2, pipeline, 0)

    def put(t, carry):
        out_ref[t] = acc[slot_ref[t]].astype(jnp.bfloat16)
        return carry

    lax.fori_loop(0, tiles, put, 0)

    def drain(j, carry):
        for step in range(1, n_st):
            send_copy(j, step).wait_send()
            return_copy(j, step).wait_send()
        for step in range(1, n_head):
            gather_copy(j, step).wait_send()
        return carry

    lax.fori_loop(0, heads, drain, 0)


def on_device(qkv_rows, out_weight, residual, source, target, window_first):
    tok_rows, three_way, feat_cols = qkv_rows.shape
    width = out_weight.shape[1]
    n_st = lax.axis_size("st")
    n_head = lax.axis_size("head")
    me = lax.axis_index("st")
    heads = feat_cols // HD
    cols = width // n_head
    tiles = tok_rows // BLK
    cap = max(2, (tiles + n_st - 1) // n_st)
    slots = n_st * cap
    total = slots * BLK

    ids = jnp.arange(tiles, dtype=jnp.int32)
    slot_ids = jnp.arange(slots, dtype=jnp.int32)
    send_block = (target.reshape(tiles, BLK)[:, 0] // tok_rows - me + n_st) % n_st
    send_rank = jnp.sum(
        ((send_block[:, None] == send_block[None, :]) & (ids[None, :] < ids[:, None])).astype(jnp.int32),
        axis=1,
    )
    send_slot = send_block * cap + send_rank
    order = jnp.sum(jnp.where(send_slot[None, :] == slot_ids[:, None], ids[None, :], 0), axis=1)
    src = source.reshape(tiles, BLK)[:, 0]
    src_block = (me - src // tok_rows + n_st) % n_st
    recv_rank = jnp.sum(
        ((src_block[:, None] == src_block[None, :]) & (src[None, :] < src[:, None])).astype(jnp.int32),
        axis=1,
    )
    recv_slot = src_block * cap + recv_rank
    window = window_first.reshape(tiles, BLK)[:, 0] // BLK - me * tiles
    wid = HD - 1 + jnp.sum(
        jnp.where(recv_slot[None, :] == slot_ids[:, None], window[None, :] - (HD - 1), 0), axis=1
    )

    dims = (n_st, n_head, heads, tiles, cap, cols)
    bf16 = jnp.bfloat16
    dma = pltpu.SemaphoreType.DMA
    smem = pl.BlockSpec(memory_space=pltpu.SMEM)
    hbm = pl.BlockSpec(memory_space=pl.ANY)
    projected = pl.pallas_call(
        functools.partial(layer_kernel, dims),
        out_shape=jax.ShapeDtypeStruct((tiles, BLK, cols), bf16),
        in_specs=[smem, smem, smem, hbm, hbm],
        out_specs=pl.BlockSpec(memory_space=pltpu.VMEM),
        scratch_shapes=[
            pltpu.VMEM((3, tiles, BLK, HD), bf16),
            pltpu.VMEM((3, tiles, BLK, HD), bf16),
            pltpu.VMEM((heads, 3, total, HD), bf16),
            pltpu.VMEM((heads, 3, total, HD), bf16),
            pltpu.VMEM((heads, total, HD), bf16),
            pltpu.VMEM((heads, total, n_head * HD), bf16),
            pltpu.VMEM((heads, n_head * HD, cols), bf16),
            pltpu.VMEM((slots, BLK, cols), jnp.float32),
            pltpu.VMEM((total, HD), bf16),
            pltpu.VMEM((total, HD), bf16),
            dma((2,)),
            dma,
            dma((heads, n_st - 1)),
            dma((heads, n_st - 1)),
            dma((heads, n_st - 1)),
            dma((heads, n_st - 1)),
            dma((heads, n_head - 1)),
            dma((heads, n_head - 1)),
            dma((n_head - 1,)),
            dma((n_head - 1,)),
        ],
        compiler_params=pltpu.CompilerParams(
            collective_id=0, has_side_effects=True, vmem_limit_bytes=60 * 1024 * 1024
        ),
    )(
        order.astype(jnp.int32),
        wid.astype(jnp.int32),
        send_slot.astype(jnp.int32),
        jnp.transpose(qkv_rows, (1, 0, 2)).reshape(three_way, tiles, BLK, feat_cols),
        out_weight.reshape(heads, HD, width),
    )
    projected = projected.reshape(tok_rows, cols)
    return (residual.astype(jnp.float32) + projected.astype(jnp.float32)).astype(bf16)


def solution(mesh):
    placed = (
        P(("group", "st"), None, "head"),
        P("head", None),
        P(("group", "st"), "head"),
        P(("group", "st")),
        P(("group", "st")),
        P(("group", "st")),
    )
    return jax.shard_map(
        on_device, mesh=mesh, in_specs=placed, out_specs=P(("group", "st"), "head"), check_vma=False
    )
```

```python
import functools
import math

import jax
import jax.numpy as jnp
from jax import lax
from jax.experimental import pallas as pl
from jax.experimental.pallas import tpu as pltpu
from jax.sharding import PartitionSpec as P

HD = 128
BLK = 64
FAR = 16384.0
DEPTH = 2
MESH = pl.DeviceIdType.MESH


def layer_kernel(
    dims,
    order_ref,
    wid_ref,
    slot_ref,
    qkv_ref,
    w_ref,
    out_ref,
    qbuf0,
    qbuf1,
    packed,
    recv,
    att,
    home,
    wbuf,
    acc,
    q_tag,
    k_tag,
    load_sem,
    wl_sem,
    qs,
    qr,
    rs,
    rr,
    gs,
    gr,
    ws,
    wr,
):
    n_st, n_head, heads, tiles, cap, cols = dims
    rows = cap * BLK
    total = n_st * rows
    my_st = lax.axis_index("st")
    my_head = lax.axis_index("head")

    def st_peer(step):
        return {"st": lax.rem(my_st + step + n_st, n_st)}

    qbufs = (qbuf0, qbuf1)

    def load_copy(j, side):
        return pltpu.make_async_copy(
            qkv_ref.at[:, :, :, pl.ds(pl.multiple_of(j * HD, HD), HD)],
            qbufs[side],
            load_sem.at[side],
        )

    def send_copy(j, step):
        part = pl.ds(step * rows, rows)
        return pltpu.make_async_remote_copy(
            src_ref=packed.at[j, :, part, :],
            dst_ref=recv.at[j, :, part, :],
            send_sem=qs.at[j, step - 1],
            recv_sem=qr.at[j, step - 1],
            device_id=st_peer(step),
            device_id_type=MESH,
        )

    def return_copy(j, step):
        part = pl.ds(step * rows, rows)
        return pltpu.make_async_remote_copy(
            src_ref=att.at[j, part, :],
            dst_ref=home.at[j, part, pl.ds(0, HD)],
            send_sem=rs.at[j, step - 1],
            recv_sem=rr.at[j, step - 1],
            device_id=st_peer(-step),
            device_id_type=MESH,
        )

    chips = n_head // 2
    my_chip = my_head // 2
    my_core = lax.rem(my_head, 2)

    def head_of(place):
        chip = lax.rem(my_chip + place // 2, chips)
        core = my_core if place % 2 == 0 else 1 - my_core
        return chip * 2 + core

    def gather_copy(j, block, place):
        at = pl.ds(pl.multiple_of(block * rows, rows), rows)
        return pltpu.make_async_remote_copy(
            src_ref=home.at[j, at, pl.ds(0, HD)],
            dst_ref=home.at[j, at, pl.ds(place * HD, HD)],
            send_sem=gs.at[j, block, place - 1],
            recv_sem=gr.at[j, block, place - 1],
            device_id={"head": head_of(place)},
            device_id_type=MESH,
        )

    def relay_copy(j, block, place):
        at = pl.ds(pl.multiple_of(block * rows, rows), rows)
        return pltpu.make_async_remote_copy(
            src_ref=home.at[j, at, pl.ds((place - 1) * HD, HD)],
            dst_ref=home.at[j, at, pl.ds(place * HD, HD)],
            send_sem=gs.at[j, block, place - 1],
            recv_sem=gr.at[j, block, place - 1],
            device_id={"head": head_of(1)},
            device_id_type=MESH,
        )

    direct = [1] + list(range(2, n_head, 2))
    relayed = list(range(3, n_head, 2))

    def gather_block(j, block):
        for place in direct:
            gather_copy(j, block, place).start()

    def weight_cols(place):
        return w_ref.at[:, :, pl.ds(pl.multiple_of(head_of(place) * cols, HD), cols)]

    def weight_copy(place):
        return pltpu.make_async_remote_copy(
            src_ref=weight_cols(place),
            dst_ref=wbuf.at[:, pl.ds(place * HD, HD), :],
            send_sem=ws.at[place - 1],
            recv_sem=wr.at[place - 1],
            device_id={"head": head_of(place)},
            device_id_type=MESH,
        )

    own_weight = pltpu.make_async_copy(weight_cols(0), wbuf.at[:, pl.ds(0, HD), :], wl_sem)

    def pack(j, side):
        load_copy(j, side).wait()
        qbuf = qbufs[side]

        def own_tile(s, carry):
            tile = order_ref[s]
            for part in range(3):
                recv[j, part, pl.ds(pl.multiple_of(s * BLK, BLK), BLK), :] = qbuf[part, tile]
            return carry

        def away_tile(s, carry):
            tile = order_ref[s]
            for part in range(3):
                packed[j, part, pl.ds(pl.multiple_of(s * BLK, BLK), BLK), :] = qbuf[part, tile]
            return carry

        lax.fori_loop(0, cap, own_tile, 0)
        lax.fori_loop(cap, n_st * cap, away_tile, 0)

    def send(j):
        for step in [n_st // 2] + [x for x in range(1, n_st) if x != n_st // 2]:
            send_copy(j, step).start()

    depth = min(DEPTH, heads)
    for j in range(min(2, heads)):
        load_copy(j, j % 2).start()
    own_weight.start()

    barrier = pltpu.get_barrier_semaphore()
    for step in range(1, n_st):
        pl.semaphore_signal(barrier, inc=1, device_id=st_peer(step), device_id_type=MESH)
    for step in range(1, n_head):
        pl.semaphore_signal(barrier, inc=1, device_id={"head": head_of(step)}, device_id_type=MESH)

    for j in range(depth):
        pack(j, j % 2)
        if j == 0:
            pl.semaphore_wait(barrier, n_st + n_head - 2)
        send(j)
        if j + 2 < heads:
            load_copy(j + 2, j % 2).start()
        if j == min(1, depth - 1):
            for step in range(1, n_head):
                weight_copy(step).start()

    lane = lax.broadcasted_iota(jnp.int32, (BLK, HD), 1)

    def tag(s, carry):
        hit = lane == wid_ref[s]
        at = pl.ds(pl.multiple_of(s * BLK, BLK), BLK)
        q_tag[at, :] = jnp.where(hit, 1.0, 0.0).astype(jnp.bfloat16)
        k_tag[at, :] = jnp.where(hit, 0.0, -FAR).astype(jnp.bfloat16)
        return carry

    lax.fori_loop(0, n_st * cap, tag, 0)
    scale = math.log2(math.e) / math.sqrt(HD)

    def attend(j, step):
        at = pl.ds(step * rows, rows)
        q = jnp.concatenate([recv[j, 0, at, :], q_tag[at, :]], axis=1)
        k = jnp.concatenate([recv[j, 1], k_tag[...]], axis=1)
        v = jnp.concatenate([recv[j, 2], jnp.ones((total, HD), jnp.bfloat16)], axis=1)
        scores = lax.dot_general(q, k, (((1,), (1,)), ((), ())), preferred_element_type=jnp.float32)
        row_max = jnp.max(scores, axis=1, keepdims=True)
        weights = jnp.exp2((scores - row_max) * scale).astype(jnp.bfloat16)
        both = jnp.dot(weights, v, preferred_element_type=jnp.float32)
        return (both[:, :HD] / both[:, HD:]).astype(jnp.bfloat16)

    def project(j, block):
        at = pl.ds(pl.multiple_of(block * rows, rows), rows)
        term = jnp.dot(home[j, at, :], wbuf[j], preferred_element_type=jnp.float32)
        acc[pl.ds(block * cap, cap)] += term.reshape(cap, BLK, cols)

    acc[...] = jnp.zeros_like(acc)

    def pipeline(t, carry):
        for side in range(2 if depth < heads else 0):

            @pl.when((t + depth < heads) & (lax.rem(t + depth, 2) == side))
            def _():
                pack(t + depth, side)
                send(t + depth)

                @pl.when(t + depth + 2 < heads)
                def _():
                    load_copy(t + depth + 2, side).start()

        @pl.when(t < heads)
        def _():
            for step in range(1, n_st):
                send_copy(t, step).wait_recv()
            for step in [n_st // 2] + [x for x in range(1, n_st) if x != n_st // 2]:
                att[t, pl.ds(step * rows, rows), :] = attend(t, step)
                return_copy(t, step).start()
            home[t, pl.ds(0, rows), pl.ds(0, HD)] = attend(t, 0)
            gather_block(t, 0)

        @pl.when((t >= 1) & (t <= heads))
        def _():
            for step in range(1, n_st):
                return_copy(t - 1, step).wait_recv()
                gather_block(t - 1, step)

        @pl.when(t == 2)
        def _():
            own_weight.wait()
            for step in range(1, n_head):
                weight_copy(step).wait()

        @pl.when(t >= 2)
        def _():
            def relay(block, carry):
                for place in relayed:
                    gather_copy(t - 2, block, place - 1).wait_recv()
                    relay_copy(t - 2, block, place).start()
                return carry

            def finish(block, carry):
                gather_copy(t - 2, block, 1).wait_recv()
                for place in relayed:
                    relay_copy(t - 2, block, place).wait_recv()
                project(t - 2, block)
                return carry

            lax.fori_loop(0, n_st, relay, 0)
            lax.fori_loop(0, n_st, finish, 0)

        return carry

    lax.fori_loop(0, heads + 2, pipeline, 0)

    def put(t, carry):
        out_ref[t] = acc[slot_ref[t]].astype(jnp.bfloat16)
        return carry

    lax.fori_loop(0, tiles, put, 0)

    def drain(j, carry):
        for step in range(1, n_st):
            send_copy(j, step).wait_send()
            return_copy(j, step).wait_send()
        for block in range(n_st):
            for place in direct:
                gather_copy(j, block, place).wait_send()
            for place in relayed:
                relay_copy(j, block, place).wait_send()
        return carry

    lax.fori_loop(0, heads, drain, 0)


def on_device(qkv_rows, out_weight, residual, source, target, window_first):
    tok_rows, three_way, feat_cols = qkv_rows.shape
    width = out_weight.shape[1]
    n_st = lax.axis_size("st")
    n_head = lax.axis_size("head")
    me = lax.axis_index("st")
    heads = feat_cols // HD
    cols = width // n_head
    tiles = tok_rows // BLK
    cap = max(2, (tiles + n_st - 1) // n_st)
    slots = n_st * cap
    total = slots * BLK

    ids = jnp.arange(tiles, dtype=jnp.int32)
    slot_ids = jnp.arange(slots, dtype=jnp.int32)
    send_block = (target.reshape(tiles, BLK)[:, 0] // tok_rows - me + n_st) % n_st
    send_rank = jnp.sum(
        ((send_block[:, None] == send_block[None, :]) & (ids[None, :] < ids[:, None])).astype(jnp.int32),
        axis=1,
    )
    send_slot = send_block * cap + send_rank
    order = jnp.sum(jnp.where(send_slot[None, :] == slot_ids[:, None], ids[None, :], 0), axis=1)
    src = source.reshape(tiles, BLK)[:, 0]
    src_block = (me - src // tok_rows + n_st) % n_st
    recv_rank = jnp.sum(
        ((src_block[:, None] == src_block[None, :]) & (src[None, :] < src[:, None])).astype(jnp.int32),
        axis=1,
    )
    recv_slot = src_block * cap + recv_rank
    window = window_first.reshape(tiles, BLK)[:, 0] // BLK - me * tiles
    wid = HD - 1 + jnp.sum(
        jnp.where(recv_slot[None, :] == slot_ids[:, None], window[None, :] - (HD - 1), 0), axis=1
    )

    dims = (n_st, n_head, heads, tiles, cap, cols)
    bf16 = jnp.bfloat16
    dma = pltpu.SemaphoreType.DMA
    smem = pl.BlockSpec(memory_space=pltpu.SMEM)
    hbm = pl.BlockSpec(memory_space=pl.ANY)
    projected = pl.pallas_call(
        functools.partial(layer_kernel, dims),
        out_shape=jax.ShapeDtypeStruct((tiles, BLK, cols), bf16),
        in_specs=[smem, smem, smem, hbm, hbm],
        out_specs=pl.BlockSpec(memory_space=pltpu.VMEM),
        scratch_shapes=[
            pltpu.VMEM((3, tiles, BLK, HD), bf16),
            pltpu.VMEM((3, tiles, BLK, HD), bf16),
            pltpu.VMEM((heads, 3, total, HD), bf16),
            pltpu.VMEM((heads, 3, total, HD), bf16),
            pltpu.VMEM((heads, total, HD), bf16),
            pltpu.VMEM((heads, total, n_head * HD), bf16),
            pltpu.VMEM((heads, n_head * HD, cols), bf16),
            pltpu.VMEM((slots, BLK, cols), jnp.float32),
            pltpu.VMEM((total, HD), bf16),
            pltpu.VMEM((total, HD), bf16),
            dma((2,)),
            dma,
            dma((heads, n_st - 1)),
            dma((heads, n_st - 1)),
            dma((heads, n_st - 1)),
            dma((heads, n_st - 1)),
            dma((heads, n_st, n_head - 1)),
            dma((heads, n_st, n_head - 1)),
            dma((n_head - 1,)),
            dma((n_head - 1,)),
        ],
        compiler_params=pltpu.CompilerParams(
            collective_id=0, has_side_effects=True, vmem_limit_bytes=60 * 1024 * 1024
        ),
    )(
        order.astype(jnp.int32),
        wid.astype(jnp.int32),
        send_slot.astype(jnp.int32),
        jnp.transpose(qkv_rows, (1, 0, 2)).reshape(three_way, tiles, BLK, feat_cols),
        out_weight.reshape(heads, HD, width),
    )
    projected = projected.reshape(tok_rows, cols)
    return (residual.astype(jnp.float32) + projected.astype(jnp.float32)).astype(bf16)


def solution(mesh):
    placed = (
        P(("group", "st"), None, "head"),
        P("head", None),
        P(("group", "st"), "head"),
        P(("group", "st")),
        P(("group", "st")),
        P(("group", "st")),
    )
    return jax.shard_map(
        on_device, mesh=mesh, in_specs=placed, out_specs=P(("group", "st"), "head"), check_vma=False
    )
```

```python
import functools
import math

import jax
import jax.numpy as jnp
from jax import lax
from jax.experimental import pallas as pl
from jax.experimental.pallas import tpu as pltpu
from jax.sharding import PartitionSpec as P

HD = 128
BLK = 64
FAR = 16384.0
DEPTH = 2
MESH = pl.DeviceIdType.MESH


def layer_kernel(
    dims,
    order_ref,
    wid_ref,
    slot_ref,
    qkv_ref,
    w_ref,
    res_ref,
    out_ref,
    qbuf0,
    qbuf1,
    packed,
    recv,
    att,
    home,
    wbuf,
    acc,
    q_tag,
    k_tag,
    res_buf,
    load_sem,
    wl_sem,
    res_sem,
    qs,
    qr,
    rs,
    rr,
    gs,
    gr,
    ws,
    wr,
):
    n_st, n_head, heads, tiles, cap, cols = dims
    rows = cap * BLK
    total = n_st * rows
    my_st = lax.axis_index("st")
    my_head = lax.axis_index("head")

    def st_peer(step):
        return {"st": lax.rem(my_st + step + n_st, n_st)}

    qbufs = (qbuf0, qbuf1)

    def load_copy(j, side):
        return pltpu.make_async_copy(
            qkv_ref.at[:, :, :, pl.ds(pl.multiple_of(j * HD, HD), HD)],
            qbufs[side],
            load_sem.at[side],
        )

    def send_copy(j, step, kind):
        part = pl.ds(step * rows, rows)
        which = pl.ds(1, 2) if kind else pl.ds(0, 1)
        return pltpu.make_async_remote_copy(
            src_ref=packed.at[j, which, part, :],
            dst_ref=recv.at[j, which, part, :],
            send_sem=qs.at[j, kind, step - 1],
            recv_sem=qr.at[j, kind, step - 1],
            device_id=st_peer(step),
            device_id_type=MESH,
        )

    def return_copy(j, step):
        part = pl.ds(step * rows, rows)
        return pltpu.make_async_remote_copy(
            src_ref=att.at[j, part, :],
            dst_ref=home.at[j, part, pl.ds(0, HD)],
            send_sem=rs.at[j, step - 1],
            recv_sem=rr.at[j, step - 1],
            device_id=st_peer(-step),
            device_id_type=MESH,
        )

    chips = n_head // 2
    my_chip = my_head // 2
    my_core = lax.rem(my_head, 2)

    def head_of(place):
        chip = lax.rem(my_chip + place // 2, chips)
        core = my_core if place % 2 == 0 else 1 - my_core
        return chip * 2 + core

    def gather_copy(j, block, place):
        at = pl.ds(pl.multiple_of(block * rows, rows), rows)
        return pltpu.make_async_remote_copy(
            src_ref=home.at[j, at, pl.ds(0, HD)],
            dst_ref=home.at[j, at, pl.ds(place * HD, HD)],
            send_sem=gs.at[j, block, place - 1],
            recv_sem=gr.at[j, block, place - 1],
            device_id={"head": head_of(place)},
            device_id_type=MESH,
        )

    def relay_copy(j, block, place):
        at = pl.ds(pl.multiple_of(block * rows, rows), rows)
        return pltpu.make_async_remote_copy(
            src_ref=home.at[j, at, pl.ds((place - 1) * HD, HD)],
            dst_ref=home.at[j, at, pl.ds(place * HD, HD)],
            send_sem=gs.at[j, block, place - 1],
            recv_sem=gr.at[j, block, place - 1],
            device_id={"head": head_of(1)},
            device_id_type=MESH,
        )

    direct = [1] + list(range(2, n_head, 2))
    relayed = list(range(3, n_head, 2))

    def gather_block(j, block):
        for place in direct:
            gather_copy(j, block, place).start()

    def weight_cols(place):
        return w_ref.at[:, :, pl.ds(pl.multiple_of(head_of(place) * cols, HD), cols)]

    def weight_copy(place):
        return pltpu.make_async_remote_copy(
            src_ref=weight_cols(place),
            dst_ref=wbuf.at[:, pl.ds(place * HD, HD), :],
            send_sem=ws.at[place - 1],
            recv_sem=wr.at[place - 1],
            device_id={"head": head_of(place)},
            device_id_type=MESH,
        )

    own_weight = pltpu.make_async_copy(weight_cols(0), wbuf.at[:, pl.ds(0, HD), :], wl_sem)

    def pack(j, side):
        load_copy(j, side).wait()
        qbuf = qbufs[side]

        def own_tile(s, carry):
            tile = order_ref[s]
            for part in range(3):
                recv[j, part, pl.ds(pl.multiple_of(s * BLK, BLK), BLK), :] = qbuf[part, tile]
            return carry

        def away_tile(s, carry):
            tile = order_ref[s]
            for part in range(3):
                packed[j, part, pl.ds(pl.multiple_of(s * BLK, BLK), BLK), :] = qbuf[part, tile]
            return carry

        lax.fori_loop(0, cap, own_tile, 0)
        lax.fori_loop(cap, n_st * cap, away_tile, 0)

    across = [n_st // 2] + [x for x in range(1, n_st) if x != n_st // 2]

    def send(j):
        for kind in (1, 0):
            for step in across:
                send_copy(j, step, kind).start()

    depth = min(DEPTH, heads)
    for j in range(min(2, heads)):
        load_copy(j, j % 2).start()
    own_weight.start()
    res_load = pltpu.make_async_copy(res_ref, res_buf, res_sem)
    res_load.start()

    barrier = pltpu.get_barrier_semaphore()
    for step in range(1, n_st):
        pl.semaphore_signal(barrier, inc=1, device_id=st_peer(step), device_id_type=MESH)
    for step in range(1, n_head):
        pl.semaphore_signal(barrier, inc=1, device_id={"head": head_of(step)}, device_id_type=MESH)

    for j in range(depth):
        pack(j, j % 2)
        if j == 0:
            pl.semaphore_wait(barrier, n_st + n_head - 2)
        send(j)
        if j + 2 < heads:
            load_copy(j + 2, j % 2).start()
        if j == min(1, depth - 1):
            for step in range(1, n_head):
                weight_copy(step).start()

    lane = lax.broadcasted_iota(jnp.int32, (BLK, HD), 1)

    def tag(s, carry):
        hit = lane == wid_ref[s]
        at = pl.ds(pl.multiple_of(s * BLK, BLK), BLK)
        q_tag[at, :] = jnp.where(hit, 1.0, 0.0).astype(jnp.bfloat16)
        k_tag[at, :] = jnp.where(hit, 0.0, -FAR).astype(jnp.bfloat16)
        return carry

    lax.fori_loop(0, n_st * cap, tag, 0)
    scale = math.log2(math.e) / math.sqrt(HD)

    def attend(j, step):
        at = pl.ds(step * rows, rows)
        q = jnp.concatenate([recv[j, 0, at, :], q_tag[at, :]], axis=1)
        k = jnp.concatenate([recv[j, 1], k_tag[...]], axis=1)
        v = jnp.concatenate([recv[j, 2], jnp.ones((total, HD), jnp.bfloat16)], axis=1)
        scores = lax.dot_general(q, k, (((1,), (1,)), ((), ())), preferred_element_type=jnp.float32)
        row_max = jnp.max(scores, axis=1, keepdims=True)
        weights = jnp.exp2((scores - row_max) * scale).astype(jnp.bfloat16)
        both = jnp.dot(weights, v, preferred_element_type=jnp.float32)
        return (both[:, :HD] / both[:, HD:]).astype(jnp.bfloat16)

    def project(j, block):
        at = pl.ds(pl.multiple_of(block * rows, rows), rows)
        term = jnp.dot(home[j, at, :], wbuf[j], preferred_element_type=jnp.float32)
        acc[pl.ds(block * cap, cap)] += term.reshape(cap, BLK, cols)

    acc[...] = jnp.zeros_like(acc)

    def pipeline(t, carry):
        for side in range(2 if depth < heads else 0):

            @pl.when((t + depth < heads) & (lax.rem(t + depth, 2) == side))
            def _():
                pack(t + depth, side)
                send(t + depth)

                @pl.when(t + depth + 2 < heads)
                def _():
                    load_copy(t + depth + 2, side).start()

        @pl.when(t < heads)
        def _():
            for step in range(1, n_st):
                send_copy(t, step, 1).wait_recv()
            home[t, pl.ds(0, rows), pl.ds(0, HD)] = attend(t, 0)
            gather_block(t, 0)
            for step in across:
                send_copy(t, step, 0).wait_recv()
                att[t, pl.ds(step * rows, rows), :] = attend(t, step)
                return_copy(t, step).start()

        @pl.when((t >= 1) & (t <= heads))
        def _():
            for step in range(1, n_st):
                return_copy(t - 1, step).wait_recv()
                gather_block(t - 1, step)

        @pl.when(t == 2)
        def _():
            own_weight.wait()
            for step in range(1, n_head):
                weight_copy(step).wait()

        @pl.when(t >= 2)
        def _():
            def relay(block, carry):
                for place in relayed:
                    gather_copy(t - 2, block, place - 1).wait_recv()
                    relay_copy(t - 2, block, place).start()
                return carry

            def finish(block, carry):
                gather_copy(t - 2, block, 1).wait_recv()
                for place in relayed:
                    relay_copy(t - 2, block, place).wait_recv()
                project(t - 2, block)
                return carry

            lax.fori_loop(0, n_st, relay, 0)
            lax.fori_loop(0, n_st, finish, 0)

        return carry

    lax.fori_loop(0, heads + 2, pipeline, 0)

    res_load.wait()

    def put(t, carry):
        out_ref[t] = (res_buf[t].astype(jnp.float32) + acc[slot_ref[t]]).astype(jnp.bfloat16)
        return carry

    lax.fori_loop(0, tiles, put, 0)

    def drain(j, carry):
        for step in range(1, n_st):
            send_copy(j, step, 0).wait_send()
            send_copy(j, step, 1).wait_send()
            return_copy(j, step).wait_send()
        for block in range(n_st):
            for place in direct:
                gather_copy(j, block, place).wait_send()
            for place in relayed:
                relay_copy(j, block, place).wait_send()
        return carry

    lax.fori_loop(0, heads, drain, 0)


def on_device(qkv_rows, out_weight, residual, source, target, window_first):
    tok_rows, three_way, feat_cols = qkv_rows.shape
    width = out_weight.shape[1]
    n_st = lax.axis_size("st")
    n_head = lax.axis_size("head")
    me = lax.axis_index("st")
    heads = feat_cols // HD
    cols = width // n_head
    tiles = tok_rows // BLK
    cap = max(2, (tiles + n_st - 1) // n_st)
    slots = n_st * cap
    total = slots * BLK

    ids = jnp.arange(tiles, dtype=jnp.int32)
    slot_ids = jnp.arange(slots, dtype=jnp.int32)
    send_block = (lax.slice(target, (0,), (tok_rows,), (BLK,)) // tok_rows - me + n_st) % n_st
    send_rank = jnp.sum(
        ((send_block[:, None] == send_block[None, :]) & (ids[None, :] < ids[:, None])).astype(jnp.int32),
        axis=1,
    )
    send_slot = send_block * cap + send_rank
    order = jnp.sum(jnp.where(send_slot[None, :] == slot_ids[:, None], ids[None, :], 0), axis=1)
    src = lax.slice(source, (0,), (tok_rows,), (BLK,))
    src_block = (me - src // tok_rows + n_st) % n_st
    recv_rank = jnp.sum(
        ((src_block[:, None] == src_block[None, :]) & (src[None, :] < src[:, None])).astype(jnp.int32),
        axis=1,
    )
    recv_slot = src_block * cap + recv_rank
    window = lax.slice(window_first, (0,), (tok_rows,), (BLK,)) // BLK - me * tiles
    wid = HD - 1 + jnp.sum(
        jnp.where(recv_slot[None, :] == slot_ids[:, None], window[None, :] - (HD - 1), 0), axis=1
    )

    dims = (n_st, n_head, heads, tiles, cap, cols)
    bf16 = jnp.bfloat16
    dma = pltpu.SemaphoreType.DMA
    smem = pl.BlockSpec(memory_space=pltpu.SMEM)
    hbm = pl.BlockSpec(memory_space=pl.ANY)
    projected = pl.pallas_call(
        functools.partial(layer_kernel, dims),
        out_shape=jax.ShapeDtypeStruct((tiles, BLK, cols), bf16),
        in_specs=[smem, smem, smem, hbm, hbm, hbm],
        out_specs=pl.BlockSpec(memory_space=pltpu.VMEM),
        scratch_shapes=[
            pltpu.VMEM((3, tiles, BLK, HD), bf16),
            pltpu.VMEM((3, tiles, BLK, HD), bf16),
            pltpu.VMEM((heads, 3, total, HD), bf16),
            pltpu.VMEM((heads, 3, total, HD), bf16),
            pltpu.VMEM((heads, total, HD), bf16),
            pltpu.VMEM((heads, total, n_head * HD), bf16),
            pltpu.VMEM((heads, n_head * HD, cols), bf16),
            pltpu.VMEM((slots, BLK, cols), jnp.float32),
            pltpu.VMEM((total, HD), bf16),
            pltpu.VMEM((total, HD), bf16),
            pltpu.VMEM((tiles, BLK, cols), bf16),
            dma((2,)),
            dma,
            dma,
            dma((heads, 2, n_st - 1)),
            dma((heads, 2, n_st - 1)),
            dma((heads, n_st - 1)),
            dma((heads, n_st - 1)),
            dma((heads, n_st, n_head - 1)),
            dma((heads, n_st, n_head - 1)),
            dma((n_head - 1,)),
            dma((n_head - 1,)),
        ],
        compiler_params=pltpu.CompilerParams(
            collective_id=0, has_side_effects=True, vmem_limit_bytes=60 * 1024 * 1024
        ),
    )(
        order.astype(jnp.int32),
        wid.astype(jnp.int32),
        send_slot.astype(jnp.int32),
        jnp.transpose(qkv_rows, (1, 0, 2)).reshape(three_way, tiles, BLK, feat_cols),
        out_weight.reshape(heads, HD, width),
        residual.reshape(tiles, BLK, cols),
    )
    return projected.reshape(tok_rows, cols)


def solution(mesh):
    placed = (
        P(("group", "st"), None, "head"),
        P("head", None),
        P(("group", "st"), "head"),
        P(("group", "st")),
        P(("group", "st")),
        P(("group", "st")),
    )
    return jax.shard_map(
        on_device, mesh=mesh, in_specs=placed, out_specs=P(("group", "st"), "head"), check_vma=False
    )
```
